32 devices in a mesh: slab: 4 (over x, core), kt: 8 (over z, y).
Axes of the slice: x: 2, y: 2, z: 4, core: 2. Of those that a mesh axis runs over, the one named last changes fastest.
Arguments:
- energies: float32 [4], replicated, may hold values from -0.5 to 0.1
- onsite: float32 [8, 4, 384], P('kt', 'slab'), may hold values from -3.5 to -2.5
- hamiltonian: bfloat16 [8, 4, 2, 384, 384], P('kt', 'slab'), may hold values from -0.109375 to 0.109375
- hopping: bfloat16 [8, 4, 2, 384, 384], P('kt', 'slab'), may hold values from -0.15625 to 0.15625
- contact: bfloat16 [8, 2, 384, 384], P('kt'), may hold values from -2 to 2
- previous: bfloat16 [8, 4, 4, 2, 2, 384, 384], P('kt', None, 'slab'), may hold values from -4 to 4
- neighbours: int32 [8, 2], P('kt'), may hold values from 0 to 7, as said below
- mode_index: int32 [8, 2], P('kt'), may hold values from 0 to 3
- mode_strength: float32 [4], replicated, may hold values from 0.25 to 1
Outputs:
- retarded: bfloat16 [8, 4, 4, 2, 384, 384], P('kt', None, 'slab')
- lesser: bfloat16 [8, 4, 4, 2, 384, 384], P('kt', None, 'slab')
The draws below stay inside these ranges and needn't reach their ends.
Inputs may be any that keep to these rules, and one draw needn't show every extreme that they name: neighbours[k, 0] is k - 1 or k - 2 and neighbours[k, 1] is k + 1 or k + 2, modulo 8.
All inputs are finite; a program needn't handle non-finite values.
Results may differ from the reference program's by a relative error of at most 0.017.
Values may be sent and summed in bfloat16 or wider, within the bound.
A program may use at most 128 MiB of HBM per device.

```python
import math
import jax
import jax.numpy as jnp
from jax import lax

B = 384
NE = 4
MODES = 4
NSL = 4
K = 8


def draw_previous(key, part):
    full_shape = (K, NE, NSL, 2, 2, B, B)
    values = jax.random.truncated_normal(key, -4.0, 4.0, full_shape, jnp.float32)
    kinds = jnp.arange(2).reshape(1, 1, 1, 2, 1, 1, 1)
    factor = jnp.where(kinds == 0, 1.0 / math.sqrt(B), 1.0)
    return (values * factor).astype(jnp.bfloat16)


def draw_contact(key, part):
    full_shape = (K, 2, B, B)
    key_off = jax.random.fold_in(key, 11)
    key_real = jax.random.fold_in(key, 12)
    key_imag = jax.random.fold_in(key, 13)
    spread = jax.random.truncated_normal(key_off, -4.0, 4.0, full_shape, jnp.float32)
    level_real = jax.random.uniform(key_real, (K, B), jnp.float32, -0.3, 0.3)
    level_imag = jnp.exp(jax.random.uniform(key_imag, (K, B), jnp.float32, math.log(0.5), math.log(1.5)))
    identity = jnp.eye(B, dtype=jnp.float32)
    diagonal_part = jnp.stack([level_real[:, :, None] * identity[None], -level_imag[:, :, None] * identity[None]], axis=1)
    values = spread * (0.5 / math.sqrt(B)) + diagonal_part
    return values.astype(jnp.bfloat16)


def draw_neighbours(key, part):
    distance = jax.random.randint(key, (K, 2), 1, 3)
    kpoints = jnp.arange(K)
    backward = (kpoints - distance[:, 0]) % K
    forward = (kpoints + distance[:, 1]) % K
    return jnp.stack([backward, forward], axis=1).astype(jnp.int32)


def touch_ends(drawn, rng, smallest, top_value):
    shape = drawn.shape
    place = [jax.random.randint(jax.random.fold_in(rng, axis), (), 0, shape[axis]) for axis in range(len(shape))]
    drawn = drawn.at[tuple(place)].set(smallest)
    longest = shape.index(max(shape))
    place[longest] = (place[longest] + 1) % shape[longest]
    return drawn.at[tuple(place)].set(top_value)


def steps_of(stream_key, shape, split, smallest, largest):
    def one(position, blocks):
        draws = jax.random.uniform(jax.random.fold_in(jax.random.fold_in(stream_key, 6), position), (blocks,), jnp.float32, smallest / len(split), largest / len(split))
        return jnp.repeat(jnp.exp(draws), shape[position] // blocks).reshape((-1,) + (1,) * (len(shape) - position - 1))

    factor_of = one(*split[0])
    for cut in split[1:]:
        factor_of = factor_of * one(*cut)
    return factor_of


def noise(key, extent, width, reach, cuts=(), kind=jnp.bfloat16):
    gain = steps_of(key, extent, cuts, -0.22, 0.18) if cuts else 1.0
    values = jax.random.normal(key, extent, jnp.float32) * width * gain
    return jnp.minimum(jnp.maximum(values, -reach), reach).astype(kind)


def setup_inputs(seed: int = 0) -> dict:
    key_of = jax.random.split(jax.random.key(seed), 10)
    return {
        "energies": jnp.clip(jax.random.uniform(key_of[0], (NE,), jnp.float32, -0.5, 0.1), -0.5, 0.1),
        "onsite": jnp.clip(-3.5 + 1.0 * jax.random.uniform(key_of[1], (K, NSL, B), jnp.float32) ** steps_of(key_of[1], (K, NSL, B), ((0, 8), (1, 4)), -0.2, 0.2), -3.5, -2.5),
        "hamiltonian": noise(key_of[2], (K, NSL, 2, B, B), (8 * B) ** -0.5, 0.109375, ((0, 8), (1, 4))),
        "hopping": noise(key_of[3], (K, NSL, 2, B, B), (4 * B) ** -0.5, 0.15625, ((0, 8), (1, 4))),
        "contact": draw_contact(jax.random.fold_in(key_of[9], 71), 0),
        "previous": draw_previous(jax.random.fold_in(key_of[9], 71), 0),
        "neighbours": draw_neighbours(jax.random.fold_in(key_of[9], 71), 0),
        "mode_index": touch_ends(jax.random.randint(key_of[7], (K, 2), 0, MODES), jax.random.fold_in(key_of[7], 1), 0, MODES - 1).astype(jnp.int32),
        "mode_strength": jnp.clip(jnp.exp(jax.random.uniform(key_of[8], (MODES,), jnp.float32, math.log(0.25), math.log(1.0))), 0.25, 1.0),
    }


broaden = 0.05
fermi_level = 0.0
thermal = 0.1


def complex_mul(first_op, second_op):
    real_real = jnp.dot(first_op[0], second_op[0], preferred_element_type=jnp.float32)
    imag_imag = jnp.dot(first_op[1], second_op[1], preferred_element_type=jnp.float32)
    real_imag = jnp.dot(first_op[0], second_op[1], preferred_element_type=jnp.float32)
    imag_real = jnp.dot(first_op[1], second_op[0], preferred_element_type=jnp.float32)
    return jnp.stack([real_real - imag_imag, real_imag + imag_real])


def adjoint(matrix):
    return jnp.stack([matrix[0].T, -matrix[1].T])


def slab_update(boundary, energy, levels, hamilton, coupling, phonon):
    conjugate = adjoint(coupling)
    moved_r = complex_mul(coupling, boundary[0]).astype(jnp.bfloat16)
    moved_l = complex_mul(coupling, boundary[1]).astype(jnp.bfloat16)
    self_retarded = complex_mul(moved_r, conjugate)
    self_lesser = complex_mul(moved_l, conjugate)
    identity = jnp.eye(levels.shape[0], dtype=jnp.float32)
    system_real = (energy - levels)[:, None] * identity - hamilton[0].astype(jnp.float32) - self_retarded[0] - phonon[0, 0]
    system_imaginary = broaden * identity - hamilton[1].astype(jnp.float32) - self_retarded[1] - phonon[0, 1]
    diagonal_real = jnp.diagonal(system_real)
    diagonal_imaginary = jnp.diagonal(system_imaginary)
    modulus = diagonal_real * diagonal_real + diagonal_imaginary * diagonal_imaginary
    inverse_real = diagonal_real / modulus
    inverse_imaginary = -diagonal_imaginary / modulus
    scaled_real = inverse_real[:, None] * system_real - inverse_imaginary[:, None] * system_imaginary
    scaled_imaginary = inverse_real[:, None] * system_imaginary + inverse_imaginary[:, None] * system_real
    sandwich_real = scaled_real * inverse_real[None, :] - scaled_imaginary * inverse_imaginary[None, :]
    sandwich_imaginary = scaled_real * inverse_imaginary[None, :] + scaled_imaginary * inverse_real[None, :]
    first_guess = jnp.stack([2.0 * jnp.diag(inverse_real) - sandwich_real, 2.0 * jnp.diag(inverse_imaginary) - sandwich_imaginary])
    first_rounded = first_guess.astype(jnp.bfloat16)
    system_rounded = jnp.stack([system_real, system_imaginary]).astype(jnp.bfloat16)
    product = complex_mul(system_rounded, first_rounded).astype(jnp.bfloat16)
    retarded = (2.0 * first_guess - complex_mul(first_rounded, product)).astype(jnp.bfloat16)
    source = (phonon[1] + self_lesser).astype(jnp.bfloat16)
    halfway = complex_mul(retarded, source).astype(jnp.bfloat16)
    lesser = complex_mul(halfway, adjoint(retarded)).astype(jnp.bfloat16)
    return retarded, lesser


def reference(energies, onsite, hamiltonian, hopping, contact, previous, neighbours, mode_index, mode_strength):
    points = neighbours.shape[0]
    slab_count = onsite.shape[1]

    def one_point(kpoint):
        neighbour_pair = neighbours[kpoint]
        chosen = mode_index[kpoint]
        strength = mode_strength[chosen]
        phonon = strength[0] * previous[neighbour_pair[0]].astype(jnp.float32) + strength[1] * previous[neighbour_pair[1]].astype(jnp.float32)
        contact_block = contact[kpoint]
        contact_float = contact_block.astype(jnp.float32)
        skew_part = jnp.stack([contact_float[0] - contact_float[0].T, contact_float[1] + contact_float[1].T])

        def one_energy(energy, phonon_energy):
            occupation = 1.0 / (1.0 + jnp.exp((energy - fermi_level) / thermal))
            boundary = jnp.stack([contact_block, (-occupation * skew_part).astype(jnp.bfloat16)])
            retarded_list = [None] * slab_count
            lesser_list = [None] * slab_count
            for slab_num in reversed(range(slab_count)):
                ret_block, les_block = slab_update(boundary, energy, onsite[kpoint, slab_num], hamiltonian[kpoint, slab_num], hopping[kpoint, slab_num], phonon_energy[slab_num])
                retarded_list[slab_num] = ret_block
                lesser_list[slab_num] = les_block
                boundary = jnp.stack([ret_block, les_block])
            return jnp.stack(retarded_list), jnp.stack(lesser_list)

        return jax.vmap(one_energy)(energies, phonon)

    retarded, lesser = lax.map(one_point, jnp.arange(points, dtype=jnp.int32))
    return retarded, lesser
```

```python
import jax
import jax.numpy as jnp
from jax import lax
from jax.sharding import PartitionSpec as P

broaden = 0.05
fermi_level = 0.0
thermal = 0.1


def from_behind(value, axis, by):
    peers = lax.axis_size(axis)
    return lax.ppermute(value, axis, [(i, (i + by) % peers) for i in range(peers)])


def as_sent(value):
    return jax.tree.map(lambda a: a.astype(jnp.bfloat16) if a.dtype == jnp.float32 else a, value)


def combine(pieces):
    real_part = pieces[..., 0, 0, :, :] - pieces[..., 1, 1, :, :]
    imaginary_part = pieces[..., 0, 1, :, :] + pieces[..., 1, 0, :, :]
    return jnp.stack([real_part, imaginary_part], axis=-3)


def complex_mul(first_op, second_op):
    return combine(
        jnp.einsum("pij,qjk->pqik", first_op, second_op, preferred_element_type=jnp.float32)
    )


def adjoint(matrix):
    return jnp.stack([matrix[0].T, -matrix[1].T])


def mul_adjoint(first_op, second_op):
    pieces = jnp.einsum("...pij,qkj->...pqik", first_op, second_op, preferred_element_type=jnp.float32)
    real_part = pieces[..., 0, 0, :, :] + pieces[..., 1, 1, :, :]
    imaginary_part = pieces[..., 1, 0, :, :] - pieces[..., 0, 1, :, :]
    return jnp.stack([real_part, imaginary_part], axis=-3)


def slab_update(boundary, energy, levels, hamilton, coupling, phonon):
    moved_blocks = combine(
        jnp.einsum("pij,sqjk->spqik", coupling, boundary, preferred_element_type=jnp.float32)
    ).astype(jnp.bfloat16)
    self_both = mul_adjoint(moved_blocks, coupling)
    self_retarded = self_both[0]
    self_lesser = self_both[1]
    size = levels.shape[0]
    on_diagonal = lax.broadcasted_iota(jnp.int32, (size, size), 0) == lax.broadcasted_iota(
        jnp.int32, (size, size), 1
    )
    system_real = (
        jnp.where(on_diagonal, (energy - levels)[:, None], 0.0)
        - hamilton[0].astype(jnp.float32)
        - self_retarded[0]
        - phonon[0, 0]
    )
    system_imaginary = (
        jnp.where(on_diagonal, broaden, 0.0)
        - hamilton[1].astype(jnp.float32)
        - self_retarded[1]
        - phonon[0, 1]
    )
    diagonal_real = jnp.sum(jnp.where(on_diagonal, system_real, 0.0), axis=1)
    diagonal_imaginary = jnp.sum(jnp.where(on_diagonal, system_imaginary, 0.0), axis=1)
    modulus = diagonal_real * diagonal_real + diagonal_imaginary * diagonal_imaginary
    inverse_real = diagonal_real / modulus
    inverse_imaginary = -diagonal_imaginary / modulus
    scaled_real = (
        inverse_real[:, None] * system_real - inverse_imaginary[:, None] * system_imaginary
    )
    scaled_imaginary = (
        inverse_real[:, None] * system_imaginary + inverse_imaginary[:, None] * system_real
    )
    sandwich_real = (
        scaled_real * inverse_real[None, :] - scaled_imaginary * inverse_imaginary[None, :]
    )
    sandwich_imaginary = (
        scaled_real * inverse_imaginary[None, :] + scaled_imaginary * inverse_real[None, :]
    )
    first_guess = jnp.stack(
        [
            jnp.where(on_diagonal, 2.0 * inverse_real[:, None], 0.0) - sandwich_real,
            jnp.where(on_diagonal, 2.0 * inverse_imaginary[:, None], 0.0) - sandwich_imaginary,
        ]
    )
    first_rounded = first_guess.astype(jnp.bfloat16)
    system_rounded = jnp.stack([system_real, system_imaginary]).astype(jnp.bfloat16)
    product = complex_mul(system_rounded, first_rounded).astype(jnp.bfloat16)
    retarded = (2.0 * first_guess - complex_mul(first_rounded, product)).astype(jnp.bfloat16)
    source = (phonon[1] + self_lesser).astype(jnp.bfloat16)
    halfway = complex_mul(retarded, source).astype(jnp.bfloat16)
    lesser = mul_adjoint(halfway, retarded).astype(jnp.bfloat16)
    return (retarded, lesser)


def sweep_energy(boundary, energy, phonon, level_all, hamilton_all, coupling_all):
    slab_count = level_all.shape[0]
    retarded_list = [None] * slab_count
    lesser_list = [None] * slab_count
    for slab_num in reversed(range(slab_count)):
        ret_block, les_block = slab_update(
            boundary,
            energy,
            level_all[slab_num],
            hamilton_all[slab_num],
            coupling_all[slab_num],
            phonon[slab_num],
        )
        retarded_list[slab_num] = ret_block
        lesser_list[slab_num] = les_block
        boundary = jnp.stack([ret_block, les_block])
    return (jnp.stack(retarded_list), jnp.stack(lesser_list), boundary)


def cycle_phonon(blocks, neighbours, mode_index, mode_strength):
    nearest = [from_behind(blocks, "kt", offset) for offset in (1, -1)]
    farther = [from_behind(blocks, "kt", offset) for offset in (2, -2)]
    kpoint = lax.axis_index("kt")
    cycle_size = lax.axis_size("kt")
    neighbour_pair = neighbours[0]
    behind = jnp.where(neighbour_pair[0] == (kpoint - 1) % cycle_size, nearest[0], farther[0])
    forward = jnp.where(neighbour_pair[1] == (kpoint + 1) % cycle_size, nearest[1], farther[1])
    mode_table = jnp.arange(mode_strength.shape[0], dtype=jnp.int32)
    strength = jnp.sum(
        jnp.where(mode_index[0][:, None] == mode_table[None, :], mode_strength[None, :], 0.0),
        axis=1,
    )
    return strength[0] * behind[0].astype(jnp.float32) + strength[1] * forward[0].astype(
        jnp.float32
    )


def starting_blocks(contact, energy_list):
    contact_block = contact[0]
    contact_float = contact_block.astype(jnp.float32)
    skew_part = jnp.stack(
        [contact_float[0] - contact_float[0].T, contact_float[1] + contact_float[1].T]
    )
    occupation = 1.0 / (1.0 + jnp.exp((energy_list - fermi_level) / thermal))
    energy_count = energy_list.shape[0]
    contact_lesser = (-occupation[:, None, None, None] * skew_part).astype(jnp.bfloat16)
    return jnp.stack(
        [jnp.broadcast_to(contact_block, (energy_count,) + contact_block.shape), contact_lesser],
        axis=1,
    )


def body(
    energies, onsite, hamiltonian, hopping, contact, previous, neighbours, mode_index, mode_strength
):
    position = lax.axis_index("slab")
    regrouped = lax.all_to_all(previous, "slab", split_axis=1, concat_axis=2, tiled=True)
    phonon_all = cycle_phonon(regrouped, neighbours, mode_index, mode_strength)
    level_whole = lax.all_gather(onsite, "slab", axis=1, tiled=True)
    hamilton_whole, coupling_whole = (
        lax.all_gather(hamiltonian, "slab", axis=1, tiled=True),
        lax.all_gather(hopping, "slab", axis=1, tiled=True),
    )
    local_count = regrouped.shape[1]
    local_energies = lax.dynamic_slice_in_dim(energies, position * local_count, local_count, 0)
    initial = starting_blocks(contact, local_energies)

    def run_whole(boundary, energy, phonon):
        return sweep_energy(
            boundary, energy, phonon, level_whole[0], hamilton_whole[0], coupling_whole[0]
        )

    retarded_local, lesser_local, unused = jax.vmap(run_whole)(initial, local_energies, phonon_all)
    retarded_all, lesser_all = (
        lax.all_to_all(
            as_sent(retarded_local[None]), "slab", split_axis=2, concat_axis=1, tiled=True
        ),
        lax.all_to_all(
            as_sent(lesser_local[None]), "slab", split_axis=2, concat_axis=1, tiled=True
        ),
    )
    return (retarded_all, lesser_all)


def solution(mesh):
    in_specs = (
        P(),
        P("kt", "slab", None),
        P("kt", "slab", None, None, None),
        P("kt", "slab", None, None, None),
        P("kt", None, None, None),
        P("kt", None, "slab", None, None, None, None),
        P("kt", None),
        P("kt", None),
        P(),
    )
    out_specs = (P("kt", None, "slab", None, None, None), P("kt", None, "slab", None, None, None))
    return jax.shard_map(body, mesh=mesh, in_specs=in_specs, out_specs=out_specs, check_vma=False)
```

```python
import jax
import jax.numpy as jnp
from jax import lax
from jax.sharding import PartitionSpec as P

broaden = 0.05
fermi_level = 0.0
thermal = 0.1


def from_behind(value, axis, by):
    peers = lax.axis_size(axis)
    return lax.ppermute(value, axis, [(i, (i + by) % peers) for i in range(peers)])


def as_sent(value):
    return jax.tree.map(lambda a: a.astype(jnp.bfloat16) if a.dtype == jnp.float32 else a, value)


def combine(pieces):
    real_part = pieces[..., 0, 0, :, :] - pieces[..., 1, 1, :, :]
    imaginary_part = pieces[..., 0, 1, :, :] + pieces[..., 1, 0, :, :]
    return jnp.stack([real_part, imaginary_part], axis=-3)


def complex_mul(first_op, second_op):
    return combine(
        jnp.einsum("pij,qjk->pqik", first_op, second_op, preferred_element_type=jnp.float32)
    )


def adjoint(matrix):
    return jnp.stack([matrix[0].T, -matrix[1].T])


def mul_adjoint(first_op, second_op):
    pieces = jnp.einsum("...pij,qkj->...pqik", first_op, second_op, preferred_element_type=jnp.float32)
    real_part = pieces[..., 0, 0, :, :] + pieces[..., 1, 1, :, :]
    imaginary_part = pieces[..., 1, 0, :, :] - pieces[..., 0, 1, :, :]
    return jnp.stack([real_part, imaginary_part], axis=-3)


def slab_update(boundary, energy, levels, hamilton, coupling, phonon):
    moved_blocks = combine(
        jnp.einsum("pij,sqjk->spqik", coupling, boundary, preferred_element_type=jnp.float32)
    ).astype(jnp.bfloat16)
    self_both = mul_adjoint(moved_blocks, coupling)
    self_retarded = self_both[0]
    self_lesser = self_both[1]
    size = levels.shape[0]
    on_diagonal = lax.broadcasted_iota(jnp.int32, (size, size), 0) == lax.broadcasted_iota(
        jnp.int32, (size, size), 1
    )
    system_real = (
        jnp.where(on_diagonal, (energy - levels)[:, None], 0.0)
        - hamilton[0].astype(jnp.float32)
        - self_retarded[0]
        - phonon[0, 0]
    )
    system_imaginary = (
        jnp.where(on_diagonal, broaden, 0.0)
        - hamilton[1].astype(jnp.float32)
        - self_retarded[1]
        - phonon[0, 1]
    )
    diagonal_real = jnp.sum(jnp.where(on_diagonal, system_real, 0.0), axis=1)
    diagonal_imaginary = jnp.sum(jnp.where(on_diagonal, system_imaginary, 0.0), axis=1)
    modulus = diagonal_real * diagonal_real + diagonal_imaginary * diagonal_imaginary
    inverse_real = diagonal_real / modulus
    inverse_imaginary = -diagonal_imaginary / modulus
    scaled_real = (
        inverse_real[:, None] * system_real - inverse_imaginary[:, None] * system_imaginary
    )
    scaled_imaginary = (
        inverse_real[:, None] * system_imaginary + inverse_imaginary[:, None] * system_real
    )
    sandwich_real = (
        scaled_real * inverse_real[None, :] - scaled_imaginary * inverse_imaginary[None, :]
    )
    sandwich_imaginary = (
        scaled_real * inverse_imaginary[None, :] + scaled_imaginary * inverse_real[None, :]
    )
    first_guess = jnp.stack(
        [
            jnp.where(on_diagonal, 2.0 * inverse_real[:, None], 0.0) - sandwich_real,
            jnp.where(on_diagonal, 2.0 * inverse_imaginary[:, None], 0.0) - sandwich_imaginary,
        ]
    )
    first_rounded = first_guess.astype(jnp.bfloat16)
    system_rounded = jnp.stack([system_real, system_imaginary]).astype(jnp.bfloat16)
    product = complex_mul(system_rounded, first_rounded).astype(jnp.bfloat16)
    retarded = (2.0 * first_guess - complex_mul(first_rounded, product)).astype(jnp.bfloat16)
    source = (phonon[1] + self_lesser).astype(jnp.bfloat16)
    halfway = complex_mul(retarded, source).astype(jnp.bfloat16)
    lesser = mul_adjoint(halfway, retarded).astype(jnp.bfloat16)
    return (retarded, lesser)


def sweep_energy(boundary, energy, phonon, level_all, hamilton_all, coupling_all):
    slab_count = level_all.shape[0]
    retarded_list = [None] * slab_count
    lesser_list = [None] * slab_count
    for slab_num in reversed(range(slab_count)):
        ret_block, les_block = slab_update(
            boundary,
            energy,
            level_all[slab_num],
            hamilton_all[slab_num],
            coupling_all[slab_num],
            phonon[slab_num],
        )
        retarded_list[slab_num] = ret_block
        lesser_list[slab_num] = les_block
        boundary = jnp.stack([ret_block, les_block])
    return (jnp.stack(retarded_list), jnp.stack(lesser_list), boundary)


def cycle_phonon(blocks, neighbours, mode_index, mode_strength):
    nearest = [from_behind(blocks, "kt", offset) for offset in (1, -1)]
    farther = [from_behind(blocks, "kt", offset) for offset in (2, -2)]
    kpoint = lax.axis_index("kt")
    cycle_size = lax.axis_size("kt")
    neighbour_pair = neighbours[0]
    behind = jnp.where(neighbour_pair[0] == (kpoint - 1) % cycle_size, nearest[0], farther[0])
    forward = jnp.where(neighbour_pair[1] == (kpoint + 1) % cycle_size, nearest[1], farther[1])
    mode_table = jnp.arange(mode_strength.shape[0], dtype=jnp.int32)
    strength = jnp.sum(
        jnp.where(mode_index[0][:, None] == mode_table[None, :], mode_strength[None, :], 0.0),
        axis=1,
    )
    return strength[0] * behind[0].astype(jnp.float32) + strength[1] * forward[0].astype(
        jnp.float32
    )


def starting_blocks(contact, energy_list):
    contact_block = contact[0]
    contact_float = contact_block.astype(jnp.float32)
    skew_part = jnp.stack(
        [contact_float[0] - contact_float[0].T, contact_float[1] + contact_float[1].T]
    )
    occupation = 1.0 / (1.0 + jnp.exp((energy_list - fermi_level) / thermal))
    energy_count = energy_list.shape[0]
    contact_lesser = (-occupation[:, None, None, None] * skew_part).astype(jnp.bfloat16)
    return jnp.stack(
        [jnp.broadcast_to(contact_block, (energy_count,) + contact_block.shape), contact_lesser],
        axis=1,
    )


def body(
    energies, onsite, hamiltonian, hopping, contact, previous, neighbours, mode_index, mode_strength
):
    position = lax.axis_index("slab")
    kind_list = []
    for kind in range(2):
        part_list = []
        for part in range(2):
            piece = previous[:, :, :, kind : kind + 1, part : part + 1]
            regrouped = lax.all_to_all(piece, "slab", split_axis=1, concat_axis=2, tiled=True)
            part_list.append(cycle_phonon(regrouped, neighbours, mode_index, mode_strength))
        kind_list.append(jnp.concatenate(part_list, axis=3))
    phonon_all = jnp.concatenate(kind_list, axis=2)
    level_whole = lax.all_gather(onsite, "slab", axis=1, tiled=True)
    hamilton_whole, coupling_whole = (
        lax.all_gather(hamiltonian, "slab", axis=1, tiled=True),
        lax.all_gather(hopping, "slab", axis=1, tiled=True),
    )
    local_count = phonon_all.shape[0]
    local_energies = lax.dynamic_slice_in_dim(energies, position * local_count, local_count, 0)
    initial = starting_blocks(contact, local_energies)

    def run_whole(boundary, energy, phonon):
        return sweep_energy(
            boundary, energy, phonon, level_whole[0], hamilton_whole[0], coupling_whole[0]
        )

    retarded_local, lesser_local, unused = jax.vmap(run_whole)(initial, local_energies, phonon_all)
    retarded_all, lesser_all = (
        lax.all_to_all(
            as_sent(retarded_local[None]), "slab", split_axis=2, concat_axis=1, tiled=True
        ),
        lax.all_to_all(
            as_sent(lesser_local[None]), "slab", split_axis=2, concat_axis=1, tiled=True
        ),
    )
    return (retarded_all, lesser_all)


def solution(mesh):
    in_specs = (
        P(),
        P("kt", "slab", None),
        P("kt", "slab", None, None, None),
        P("kt", "slab", None, None, None),
        P("kt", None, None, None),
        P("kt", None, "slab", None, None, None, None),
        P("kt", None),
        P("kt", None),
        P(),
    )
    out_specs = (P("kt", None, "slab", None, None, None), P("kt", None, "slab", None, None, None))
    return jax.shard_map(body, mesh=mesh, in_specs=in_specs, out_specs=out_specs, check_vma=False)
```

```python
import jax
import jax.numpy as jnp
from jax import lax
from jax.sharding import PartitionSpec as P

broaden = 0.05
fermi_level = 0.0
thermal = 0.1


def from_behind(value, axis, by):
    peers = lax.axis_size(axis)
    return lax.ppermute(value, axis, [(i, (i + by) % peers) for i in range(peers)])


def as_sent(value):
    return jax.tree.map(lambda a: a.astype(jnp.bfloat16) if a.dtype == jnp.float32 else a, value)


def combine(pieces):
    real_part = pieces[..., 0, 0, :, :] - pieces[..., 1, 1, :, :]
    imaginary_part = pieces[..., 0, 1, :, :] + pieces[..., 1, 0, :, :]
    return jnp.stack([real_part, imaginary_part], axis=-3)


def complex_mul(first_op, second_op):
    return combine(
        jnp.einsum("pij,qjk->pqik", first_op, second_op, preferred_element_type=jnp.float32)
    )


def adjoint(matrix):
    return jnp.stack([matrix[0].T, -matrix[1].T])


def mul_adjoint(first_op, second_op):
    pieces = jnp.einsum("...pij,qkj->...pqik", first_op, second_op, preferred_element_type=jnp.float32)
    real_part = pieces[..., 0, 0, :, :] + pieces[..., 1, 1, :, :]
    imaginary_part = pieces[..., 1, 0, :, :] - pieces[..., 0, 1, :, :]
    return jnp.stack([real_part, imaginary_part], axis=-3)


def slab_update(boundary, energy, levels, hamilton, coupling, phonon):
    moved_blocks = combine(
        jnp.einsum("pij,sqjk->spqik", coupling, boundary, preferred_element_type=jnp.float32)
    ).astype(jnp.bfloat16)
    self_both = mul_adjoint(moved_blocks, coupling)
    self_retarded = self_both[0]
    self_lesser = self_both[1]
    size = levels.shape[0]
    on_diagonal = lax.broadcasted_iota(jnp.int32, (size, size), 0) == lax.broadcasted_iota(
        jnp.int32, (size, size), 1
    )
    system_real = (
        jnp.where(on_diagonal, (energy - levels)[:, None], 0.0)
        - hamilton[0].astype(jnp.float32)
        - self_retarded[0]
        - phonon[0, 0]
    )
    system_imaginary = (
        jnp.where(on_diagonal, broaden, 0.0)
        - hamilton[1].astype(jnp.float32)
        - self_retarded[1]
        - phonon[0, 1]
    )
    diagonal_real = jnp.sum(jnp.where(on_diagonal, system_real, 0.0), axis=1)
    diagonal_imaginary = jnp.sum(jnp.where(on_diagonal, system_imaginary, 0.0), axis=1)
    modulus = diagonal_real * diagonal_real + diagonal_imaginary * diagonal_imaginary
    inverse_real = diagonal_real / modulus
    inverse_imaginary = -diagonal_imaginary / modulus
    scaled_real = (
        inverse_real[:, None] * system_real - inverse_imaginary[:, None] * system_imaginary
    )
    scaled_imaginary = (
        inverse_real[:, None] * system_imaginary + inverse_imaginary[:, None] * system_real
    )
    sandwich_real = (
        scaled_real * inverse_real[None, :] - scaled_imaginary * inverse_imaginary[None, :]
    )
    sandwich_imaginary = (
        scaled_real * inverse_imaginary[None, :] + scaled_imaginary * inverse_real[None, :]
    )
    first_guess = jnp.stack(
        [
            jnp.where(on_diagonal, 2.0 * inverse_real[:, None], 0.0) - sandwich_real,
            jnp.where(on_diagonal, 2.0 * inverse_imaginary[:, None], 0.0) - sandwich_imaginary,
        ]
    )
    first_rounded = first_guess.astype(jnp.bfloat16)
    system_rounded = jnp.stack([system_real, system_imaginary]).astype(jnp.bfloat16)
    product = complex_mul(system_rounded, first_rounded).astype(jnp.bfloat16)
    retarded = (2.0 * first_guess - complex_mul(first_rounded, product)).astype(jnp.bfloat16)
    source = (phonon[1] + self_lesser).astype(jnp.bfloat16)
    halfway = complex_mul(retarded, source).astype(jnp.bfloat16)
    lesser = mul_adjoint(halfway, retarded).astype(jnp.bfloat16)
    return (retarded, lesser)


def sweep_energy(boundary, energy, phonon, level_all, hamilton_all, coupling_all):
    slab_count = level_all.shape[0]
    retarded_list = [None] * slab_count
    lesser_list = [None] * slab_count
    for slab_num in reversed(range(slab_count)):
        ret_block, les_block = slab_update(
            boundary,
            energy,
            level_all[slab_num],
            hamilton_all[slab_num],
            coupling_all[slab_num],
            phonon[slab_num],
        )
        retarded_list[slab_num] = ret_block
        lesser_list[slab_num] = les_block
        boundary = jnp.stack([ret_block, les_block])
    return (jnp.stack(retarded_list), jnp.stack(lesser_list), boundary)


def cycle_phonon(blocks, neighbours, mode_index, mode_strength):
    nearest = [from_behind(blocks, "kt", offset) for offset in (1, -1)]
    farther = [from_behind(blocks, "kt", offset) for offset in (2, -2)]
    kpoint = lax.axis_index("kt")
    cycle_size = lax.axis_size("kt")
    neighbour_pair = neighbours[0]
    behind = jnp.where(neighbour_pair[0] == (kpoint - 1) % cycle_size, nearest[0], farther[0])
    forward = jnp.where(neighbour_pair[1] == (kpoint + 1) % cycle_size, nearest[1], farther[1])
    mode_table = jnp.arange(mode_strength.shape[0], dtype=jnp.int32)
    strength = jnp.sum(
        jnp.where(mode_index[0][:, None] == mode_table[None, :], mode_strength[None, :], 0.0),
        axis=1,
    )
    return strength, behind, forward


def weigh(strength, behind, forward):
    return strength[0] * behind.astype(jnp.float32) + strength[1] * forward.astype(jnp.float32)


def starting_blocks(contact, energy_list):
    contact_block = contact[0]
    contact_float = contact_block.astype(jnp.float32)
    skew_part = jnp.stack(
        [contact_float[0] - contact_float[0].T, contact_float[1] + contact_float[1].T]
    )
    occupation = 1.0 / (1.0 + jnp.exp((energy_list - fermi_level) / thermal))
    energy_count = energy_list.shape[0]
    contact_lesser = (-occupation[:, None, None, None] * skew_part).astype(jnp.bfloat16)
    return jnp.stack(
        [jnp.broadcast_to(contact_block, (energy_count,) + contact_block.shape), contact_lesser],
        axis=1,
    )


def body(
    energies, onsite, hamiltonian, hopping, contact, previous, neighbours, mode_index, mode_strength
):
    position = lax.axis_index("slab")
    kind_list = []
    for kind in range(2):
        part_list = []
        for part in range(2):
            piece = previous[:, :, :, kind : kind + 1, part : part + 1]
            if kind == 0 and part == 0:
                strength, behind, forward = cycle_phonon(
                    piece, neighbours, mode_index, mode_strength
                )
                chosen = lax.all_to_all(
                    jnp.stack([behind, forward], axis=1),
                    "slab",
                    split_axis=2,
                    concat_axis=3,
                    tiled=True,
                )
                part_list.append(weigh(strength, chosen[0, 0], chosen[0, 1]))
            else:
                regrouped = lax.all_to_all(
                    piece, "slab", split_axis=1, concat_axis=2, tiled=True
                )
                strength, behind, forward = cycle_phonon(
                    regrouped, neighbours, mode_index, mode_strength
                )
                part_list.append(weigh(strength, behind[0], forward[0]))
        kind_list.append(jnp.concatenate(part_list, axis=3))
    phonon_all = jnp.concatenate(kind_list, axis=2)
    level_whole = lax.all_gather(onsite, "slab", axis=1, tiled=True)
    hamilton_whole, coupling_whole = (
        lax.all_gather(hamiltonian, "slab", axis=1, tiled=True),
        lax.all_gather(hopping, "slab", axis=1, tiled=True),
    )
    local_count = phonon_all.shape[0]
    local_energies = lax.dynamic_slice_in_dim(energies, position * local_count, local_count, 0)
    initial = starting_blocks(contact, local_energies)

    def run_whole(boundary, energy, phonon):
        return sweep_energy(
            boundary, energy, phonon, level_whole[0], hamilton_whole[0], coupling_whole[0]
        )

    retarded_local, lesser_local, unused = jax.vmap(run_whole)(initial, local_energies, phonon_all)
    both_all = lax.all_to_all(
        as_sent(jnp.stack([retarded_local, lesser_local])[:, None]),
        "slab",
        split_axis=3,
        concat_axis=2,
        tiled=True,
    )
    return (both_all[0], both_all[1])


def solution(mesh):
    in_specs = (
        P(),
        P("kt", "slab", None),
        P("kt", "slab", None, None, None),
        P("kt", "slab", None, None, None),
        P("kt", None, None, None),
        P("kt", None, "slab", None, None, None, None),
        P("kt", None),
        P("kt", None),
        P(),
    )
    out_specs = (P("kt", None, "slab", None, None, None), P("kt", None, "slab", None, None, None))
    return jax.shard_map(body, mesh=mesh, in_specs=in_specs, out_specs=out_specs, check_vma=False)
```

```python
import jax
import jax.numpy as jnp
from jax import lax
from jax.sharding import PartitionSpec as P

broaden = 0.05
fermi_level = 0.0
thermal = 0.1


def from_behind(value, axis, by):
    peers = lax.axis_size(axis)
    return lax.ppermute(value, axis, [(i, (i + by) % peers) for i in range(peers)])


def as_sent(value):
    return jax.tree.map(lambda a: a.astype(jnp.bfloat16) if a.dtype == jnp.float32 else a, value)


def combine(pieces):
    real_part = pieces[..., 0, 0, :, :] - pieces[..., 1, 1, :, :]
    imaginary_part = pieces[..., 0, 1, :, :] + pieces[..., 1, 0, :, :]
    return jnp.stack([real_part, imaginary_part], axis=-3)


def complex_mul(first_op, second_op):
    return combine(
        jnp.einsum("pij,qjk->pqik", first_op, second_op, preferred_element_type=jnp.float32)
    )


def adjoint(matrix):
    return jnp.stack([matrix[0].T, -matrix[1].T])


def mul_adjoint(first_op, second_op):
    pieces = jnp.einsum("...pij,qkj->...pqik", first_op, second_op, preferred_element_type=jnp.float32)
    real_part = pieces[..., 0, 0, :, :] + pieces[..., 1, 1, :, :]
    imaginary_part = pieces[..., 1, 0, :, :] - pieces[..., 0, 1, :, :]
    return jnp.stack([real_part, imaginary_part], axis=-3)


def slab_update(boundary, energy, levels, hamilton, coupling, phonon):
    moved_blocks = combine(
        jnp.einsum("pij,sqjk->spqik", coupling, boundary, preferred_element_type=jnp.float32)
    ).astype(jnp.bfloat16)
    self_both = mul_adjoint(moved_blocks, coupling)
    self_retarded = self_both[0]
    self_lesser = self_both[1]
    size = levels.shape[0]
    on_diagonal = lax.broadcasted_iota(jnp.int32, (size, size), 0) == lax.broadcasted_iota(
        jnp.int32, (size, size), 1
    )
    system_real = (
        jnp.where(on_diagonal, (energy - levels)[:, None], 0.0)
        - hamilton[0].astype(jnp.float32)
        - self_retarded[0]
        - phonon[0, 0]
    )
    system_imaginary = (
        jnp.where(on_diagonal, broaden, 0.0)
        - hamilton[1].astype(jnp.float32)
        - self_retarded[1]
        - phonon[0, 1]
    )
    diagonal_real = jnp.sum(jnp.where(on_diagonal, system_real, 0.0), axis=1)
    diagonal_imaginary = jnp.sum(jnp.where(on_diagonal, system_imaginary, 0.0), axis=1)
    modulus = diagonal_real * diagonal_real + diagonal_imaginary * diagonal_imaginary
    inverse_real = diagonal_real / modulus
    inverse_imaginary = -diagonal_imaginary / modulus
    scaled_real = (
        inverse_real[:, None] * system_real - inverse_imaginary[:, None] * system_imaginary
    )
    scaled_imaginary = (
        inverse_real[:, None] * system_imaginary + inverse_imaginary[:, None] * system_real
    )
    sandwich_real = (
        scaled_real * inverse_real[None, :] - scaled_imaginary * inverse_imaginary[None, :]
    )
    sandwich_imaginary = (
        scaled_real * inverse_imaginary[None, :] + scaled_imaginary * inverse_real[None, :]
    )
    first_guess = jnp.stack(
        [
            jnp.where(on_diagonal, 2.0 * inverse_real[:, None], 0.0) - sandwich_real,
            jnp.where(on_diagonal, 2.0 * inverse_imaginary[:, None], 0.0) - sandwich_imaginary,
        ]
    )
    first_rounded = first_guess.astype(jnp.bfloat16)
    system_rounded = jnp.stack([system_real, system_imaginary]).astype(jnp.bfloat16)
    product = complex_mul(system_rounded, first_rounded).astype(jnp.bfloat16)
    retarded = (2.0 * first_guess - complex_mul(first_rounded, product)).astype(jnp.bfloat16)
    source = (phonon[1] + self_lesser).astype(jnp.bfloat16)
    halfway = complex_mul(retarded, source).astype(jnp.bfloat16)
    lesser = mul_adjoint(halfway, retarded).astype(jnp.bfloat16)
    return (retarded, lesser)


def sweep_energy(boundary, energy, phonon, level_all, hamilton_all, coupling_all):
    slab_count = level_all.shape[0]
    retarded_list = [None] * slab_count
    lesser_list = [None] * slab_count
    for slab_num in reversed(range(slab_count)):
        ret_block, les_block = slab_update(
            boundary,
            energy,
            level_all[slab_num],
            hamilton_all[slab_num],
            coupling_all[slab_num],
            phonon[slab_num],
        )
        retarded_list[slab_num] = ret_block
        lesser_list[slab_num] = les_block
        boundary = jnp.stack([ret_block, les_block])
    return (jnp.stack(retarded_list), jnp.stack(lesser_list), boundary)


def cycle_phonon(blocks, neighbours, mode_index, mode_strength):
    nearest = [from_behind(blocks, "kt", offset) for offset in (1, -1)]
    farther = [from_behind(blocks, "kt", offset) for offset in (2, -2)]
    kpoint = lax.axis_index("kt")
    cycle_size = lax.axis_size("kt")
    neighbour_pair = neighbours[0]
    behind = jnp.where(neighbour_pair[0] == (kpoint - 1) % cycle_size, nearest[0], farther[0])
    forward = jnp.where(neighbour_pair[1] == (kpoint + 1) % cycle_size, nearest[1], farther[1])
    mode_table = jnp.arange(mode_strength.shape[0], dtype=jnp.int32)
    strength = jnp.sum(
        jnp.where(mode_index[0][:, None] == mode_table[None, :], mode_strength[None, :], 0.0),
        axis=1,
    )
    return strength, behind, forward


def weigh(strength, behind, forward):
    return strength[0] * behind.astype(jnp.float32) + strength[1] * forward.astype(jnp.float32)


def starting_blocks(contact, energy_list):
    contact_block = contact[0]
    contact_float = contact_block.astype(jnp.float32)
    skew_part = jnp.stack(
        [contact_float[0] - contact_float[0].T, contact_float[1] + contact_float[1].T]
    )
    occupation = 1.0 / (1.0 + jnp.exp((energy_list - fermi_level) / thermal))
    energy_count = energy_list.shape[0]
    contact_lesser = (-occupation[:, None, None, None] * skew_part).astype(jnp.bfloat16)
    return jnp.stack(
        [jnp.broadcast_to(contact_block, (energy_count,) + contact_block.shape), contact_lesser],
        axis=1,
    )


def body(
    energies, onsite, hamiltonian, hopping, contact, previous, neighbours, mode_index, mode_strength
):
    position = lax.axis_index("slab")
    half = previous.shape[5] // 2
    halves = [
        lax.all_to_all(
            previous[:, :, :, :, :, h * half : (h + 1) * half],
            "slab",
            split_axis=1,
            concat_axis=2,
            tiled=True,
        )
        for h in range(2)
    ]
    slab_total = halves[0].shape[2]
    slab_list = [None] * slab_total
    for slab_num in reversed(range(slab_total)):
        row_list = []
        for regrouped in halves:
            strength, behind, forward = cycle_phonon(
                regrouped[:, :, slab_num : slab_num + 1], neighbours, mode_index, mode_strength
            )
            row_list.append(weigh(strength, behind[0], forward[0]))
        slab_list[slab_num] = jnp.concatenate(row_list, axis=4)
    phonon_all = jnp.concatenate(slab_list, axis=1)
    level_whole = lax.all_gather(onsite, "slab", axis=1, tiled=True)
    hamilton_whole, coupling_whole = (
        lax.all_gather(hamiltonian, "slab", axis=1, tiled=True),
        lax.all_gather(hopping, "slab", axis=1, tiled=True),
    )
    local_count = phonon_all.shape[0]
    local_energies = lax.dynamic_slice_in_dim(energies, position * local_count, local_count, 0)
    initial = starting_blocks(contact, local_energies)

    def run_whole(boundary, energy, phonon):
        return sweep_energy(
            boundary, energy, phonon, level_whole[0], hamilton_whole[0], coupling_whole[0]
        )

    retarded_local, lesser_local, unused = jax.vmap(run_whole)(initial, local_energies, phonon_all)
    both_all = lax.all_to_all(
        as_sent(jnp.stack([retarded_local, lesser_local])[:, None]),
        "slab",
        split_axis=3,
        concat_axis=2,
        tiled=True,
    )
    return (both_all[0], both_all[1])


def solution(mesh):
    in_specs = (
        P(),
        P("kt", "slab", None),
        P("kt", "slab", None, None, None),
        P("kt", "slab", None, None, None),
        P("kt", None, None, None),
        P("kt", None, "slab", None, None, None, None),
        P("kt", None),
        P("kt", None),
        P(),
    )
    out_specs = (P("kt", None, "slab", None, None, None), P("kt", None, "slab", None, None, None))
    return jax.shard_map(body, mesh=mesh, in_specs=in_specs, out_specs=out_specs, check_vma=False)
```
